256 devices in a mesh: seq: 64 (over y_lo, z, x), head: 4 (over y_hi, core).
Axes of the slice: x: 4, y: 4 (y_hi: 2, y_lo: 2; y = y_hi * 2 + y_lo), z: 8, core: 2. Of those that a mesh axis runs over, the one named last changes fastest.
Arguments:
- qkv: bfloat16 [3, 64, 512, 4096], P(None, 'seq', None, 'head'), may hold values from -6 to 6
- out_weight: bfloat16 [4096, 4096], P('head', 'seq'), may hold values from -0.09375 to 0.09375
Outputs:
- layer_out: bfloat16 [512, 64, 4096], P('head', 'seq')
The draws below stay inside these ranges and needn't reach their ends.
All inputs are finite; a program needn't handle non-finite values.
Results may differ from the reference program's by a relative error of at most 0.017.
Values may be sent and summed in bfloat16 or wider, within the bound.
A program may use at most 128 MiB of HBM per device.

```python
import math
import jax
import jax.numpy as jnp
from jax import lax

HEADS = 32
HEAD = 128
D = 4096
COLS = 512
ROWS = 64


def draw_qkv(key, part):
    shape = (3, ROWS, COLS, HEADS * HEAD)
    keys = jax.random.split(key, 6)
    drawn = jax.random.normal(keys[5], shape, jnp.float32)
    return jnp.clip(drawn, -6.0, 6.0).astype(jnp.bfloat16)


def levels(key, shape, cuts, least, top_value):
    def one(position, shards_of):
        heights = jax.random.uniform(jax.random.fold_in(jax.random.fold_in(key, 6), position), (shards_of,), jnp.float32, least / len(cuts), top_value / len(cuts))
        return jnp.repeat(jnp.exp(heights), shape[position] // shards_of).reshape((-1,) + (1,) * (len(shape) - position - 1))

    level = one(*cuts[0])
    for cut in cuts[1:]:
        level = level * one(*cut)
    return level


def bell_draw(key, extent, deviation, most, cuts=(), kind=jnp.bfloat16):
    array = deviation * jax.random.normal(key, extent, jnp.float32)
    if cuts:
        array = array * levels(key, extent, cuts, -0.22, 0.18)
    return jnp.clip(array, -most, most).astype(kind)


def setup_inputs(seed: int = 0) -> dict:
    splits = jax.random.split(jax.random.key(seed), 3)
    return {
        "qkv": draw_qkv(jax.random.fold_in(splits[2], 71), 0),
        "out_weight": bell_draw(splits[1], (HEADS * HEAD, D), (HEADS * HEAD) ** -0.5, 0.09375, ((0, 4), (1, 64))),
    }


def to_bf16_f32(values):
    return lax.optimization_barrier(values.astype(jnp.bfloat16)).astype(jnp.float32)

def reference(qkv, out_weight):
    scale = 1.0 / math.sqrt(HEAD)
    whole = qkv.reshape(3, ROWS, COLS, HEADS, HEAD)
    zero_row = jnp.zeros((2, 1, COLS, HEADS, HEAD), qkv.dtype)
    keys_ext = jnp.concatenate([zero_row, whole[1:3]], axis=1)
    key_idx = lax.broadcasted_iota(jnp.int32, (COLS, 2 * COLS), 1)
    query_idx = lax.broadcasted_iota(jnp.int32, (COLS, 2 * COLS), 0)

    def one_row(index):
        queries = lax.dynamic_index_in_dim(whole[0], index, 0, keepdims=False).astype(jnp.float32)
        pair = lax.dynamic_slice_in_dim(keys_ext, index, 2, axis=1).reshape(2, 2 * COLS, HEADS, HEAD).astype(jnp.float32)
        scores = jnp.einsum('qhd,khd->hqk', queries, pair[0]) * scale
        allowed = (key_idx < COLS) & (index > 0) | (key_idx >= COLS) & (key_idx - COLS <= query_idx)
        masked = jnp.where(allowed[None], scores, jnp.float32(-1e+30))
        peak = lax.optimization_barrier(jnp.max(masked, axis=-1))
        weights = jnp.where(allowed[None], jnp.exp(masked - peak[..., None]), jnp.float32(0.0))
        total = lax.optimization_barrier(jnp.sum(weights, axis=-1))
        mixed = jnp.einsum('hqk,khd->qhd', to_bf16_f32(weights), pair[1])
        row_out = mixed / jnp.transpose(total)[..., None]
        row_lse = jnp.transpose(peak + jnp.log(total))
        return (row_out, row_lse)
    row_out, row_lse = lax.map(one_row, jnp.arange(ROWS, dtype=jnp.int32))
    r_idx = lax.broadcasted_iota(jnp.int32, (ROWS, ROWS), 0)
    s_idx = lax.broadcasted_iota(jnp.int32, (ROWS, ROWS), 1)
    col_allowed = s_idx <= r_idx - 2

    def one_head(head):
        part = lax.dynamic_index_in_dim(whole, head, 3, keepdims=False).astype(jnp.float32)
        scores = jnp.einsum('rcd,scd->crs', part[0], part[1]) * scale
        masked = jnp.where(col_allowed[None], scores, jnp.float32(-1e+30))
        peak = lax.optimization_barrier(jnp.max(masked, axis=-1))
        weights = jnp.where(col_allowed[None], jnp.exp(masked - peak[..., None]), jnp.float32(0.0))
        total = jnp.maximum(lax.optimization_barrier(jnp.sum(weights, axis=-1)), jnp.float32(1.0))
        mixed = jnp.einsum('crs,scd->rcd', to_bf16_f32(weights), part[2])
        col_out = to_bf16_f32(mixed / jnp.transpose(total)[..., None])
        col_lse = jnp.transpose(peak + jnp.log(total))
        return (col_out, col_lse)
    col_out, col_lse = lax.map(one_head, jnp.arange(HEADS, dtype=jnp.int32))
    col_out = jnp.moveaxis(col_out, 0, 2)
    col_lse = jnp.moveaxis(col_lse, 0, 2)
    top = jnp.maximum(row_lse, col_lse)
    left = jnp.exp(row_lse - top)
    right = jnp.exp(col_lse - top)
    attended = (left[..., None] * row_out + right[..., None] * col_out) / (left + right)[..., None]
    attended = attended.astype(jnp.bfloat16).reshape(ROWS * COLS, HEADS * HEAD)
    projected = jnp.dot(attended, out_weight, preferred_element_type=jnp.float32).astype(jnp.bfloat16)
    return jnp.transpose(projected.reshape(ROWS, COLS, D), (1, 0, 2))
```

```python
import functools

import jax
import jax.numpy as jnp
from jax import lax
from jax.experimental import pallas as pl
from jax.experimental.pallas import tpu as pltpu
from jax.sharding import PartitionSpec as P

MESH = pl.DeviceIdType.MESH
NY, NZ, NX = 2, 8, 4
SEQ = NY * NZ * NX
C = 512
F = 1024
HEAD = 128
HL = F // HEAD
D = 4096
SLICE = D // SEQ
TOK = C // SEQ
PH = 4
PW = F // PH
HPP = HL // PH
NCH = 8
CW = D // NCH
SCALE = HEAD ** -0.5
LOG2E = 1.4426950408889634
NEG = -1e30
f32 = jnp.float32
bf16 = jnp.bfloat16


def attend(q, k, v, bias):
    s = lax.dot_general(q, k, (((1,), (1,)), ((), ())), preferred_element_type=f32)
    if bias is not None:
        s = s + bias
    m = jnp.max(s, axis=1, keepdims=True)
    p = jnp.exp2((s - m) * (SCALE * LOG2E))
    l = jnp.sum(p, axis=1, keepdims=True)
    o = jnp.dot(p.astype(bf16), v, preferred_element_type=f32) * (1.0 / l)
    return o, m * SCALE + jnp.log(l)


def put_lane(ref, rows, h, val):
    lane = lax.broadcasted_iota(jnp.int32, (val.shape[0], 128), 1)
    ref[rows, :] = jnp.where(lane == h, val, ref[rows, :])


def kernel(qkv, wt, out, loc, recv, qn, ops, lps, opr, lpr, ocs, lcs, ocr, lcr, oown, lown, wg, att,
           bown, bcol, cs, cr, own, ys, yr, ld_sem, in_s, in_r, q_s, q_r, op_s, op_r, oc_s, oc_r,
           lc_s, lc_r, w_s, w_r, c_s, c_r, y_s, y_r):
    me = lax.axis_index("seq")
    hd = lax.axis_index("head")
    yl, z, x = me // (NZ * NX), (me // NX) % NZ, me % NX
    b, c = hd // 2, hd % 2
    core_peer = {"head": b * 2 + (1 - c)}
    y_peer = {"head": (1 - b) * 2 + c}
    nxt, prv = (me + 1) % SEQ, (me + SEQ - 1) % SEQ

    def rc(src, dst, s, r, dev):
        return pltpu.make_async_remote_copy(src_ref=src, dst_ref=dst, send_sem=s, recv_sem=r,
                                            device_id=dev, device_id_type=MESH)

    barrier = pltpu.get_barrier_semaphore()

    def greet(i, _):
        pl.semaphore_signal(barrier, inc=1, device_id={"seq": (me + i) % SEQ}, device_id_type=MESH)
        return 0

    ld = pltpu.make_async_copy(qkv, loc, ld_sem.at[0])
    ld.start()
    lw = pltpu.make_async_copy(wt, wg.at[yl, z, x], w_r.at[0])
    lw.start()
    lax.fori_loop(1, SEQ, greet, 0)
    pl.semaphore_signal(barrier, inc=1, device_id=core_peer, device_id_type=MESH)
    pl.semaphore_signal(barrier, inc=1, device_id=y_peer, device_id_type=MESH)
    pl.semaphore_wait(barrier, SEQ + 1)

    qcp = rc(qkv.at[0], qn, q_s, q_r, {"seq": prv})
    qcp.start()

    def wz(i, _):
        p = (z + i) % NZ
        rc(wt, wg.at[yl, z, x], w_s.at[0], w_r.at[0], {"seq": (yl * NZ + p) * NX + x}).start()
        return 0

    lax.fori_loop(1, NZ, wz, 0)

    mine = pl.ds(pl.multiple_of(me * TOK, TOK), TOK)
    for ph in range(PH):
        lanes = pl.ds(ph * PW, PW)

        def send(i, _):
            p = (me + i) % SEQ
            rows = pl.ds(pl.multiple_of(p * TOK, TOK), TOK)
            rc(qkv.at[:, rows, lanes], recv.at[:, mine, lanes], in_s.at[ph], in_r.at[ph], {"seq": p}).start()
            return 0

        lax.fori_loop(1, SEQ, send, 0)
        pltpu.make_async_copy(qkv.at[:, mine, lanes], recv.at[:, mine, lanes], in_r.at[ph]).start()

    d = (lax.broadcasted_iota(jnp.int32, (C, C), 0) - lax.broadcasted_iota(jnp.int32, (C, C), 1))
    bown[...] = jnp.where(d >= 0, 0.0, NEG).astype(f32)
    bcol[...] = jnp.where((d >= 2 * TOK) & (d % TOK == 0), 0.0, NEG).astype(f32)
    lown[...] = jnp.zeros((C, 128), f32)
    lps[...] = jnp.zeros((C, 128), f32)
    lcs[...] = jnp.zeros((C, 128), f32)
    ld.wait()

    def head_lanes(h):
        return pl.ds(pl.multiple_of(h * HEAD, HEAD), HEAD)

    B = 256

    def own_head(h, _):
        hs = head_lanes(h)
        for i in range(C // B):
            rows, n = pl.ds(i * B, B), (i + 1) * B
            o, lse = attend(loc[0, rows, hs], loc[1, :n, hs], loc[2, :n, hs], bown[rows, :n])
            oown[rows, hs] = o
            put_lane(lown, rows, h, lse)
        return 0

    lax.fori_loop(0, HL, own_head, 0)

    pltpu.make_async_copy(wg.at[yl, :, x], wg.at[yl, :, x], w_r.at[0]).wait()
    xr, xl = (x + 1) % NX, (x + NX - 1) % NX
    to_y = {"seq": ((1 - yl) * NZ + z) * NX + x}
    to_r = {"seq": (yl * NZ + z) * NX + xr}
    to_l = {"seq": (yl * NZ + z) * NX + xl}
    H = NZ // 2
    Q = NZ // 4
    lo, hi = pl.ds(0, H), pl.ds(H, H)

    def same(ref, i, dev):
        return rc(ref, ref, w_s.at[i], w_r.at[i], dev)

    a_y = same(wg.at[yl, lo, x], 1, to_y)
    b_r = same(wg.at[yl, hi, x], 2, to_r)
    b_l = same(wg.at[yl, hi, x], 3, to_l)
    a_y.start()
    b_r.start()
    b_l.start()

    qcp.wait_recv()

    def prev_head(h, _):
        hs = head_lanes(h)
        for i in range(C // B):
            rows = pl.ds(i * B, B)
            o, lse = attend(qn[rows, hs], loc[1, :, hs], loc[2, :, hs], None)
            ops[rows, hs] = o.astype(bf16)
            put_lane(lps, rows, h, lse)
        return 0

    lax.fori_loop(0, HL, prev_head, 0)
    op = rc(ops, opr, op_s.at[0], op_r.at[0], {"seq": nxt})
    lp = rc(lps, lpr, op_s.at[1], op_r.at[1], {"seq": nxt})
    op.start()
    lp.start()

    def w_step2():
        a_y.wait_recv()
        r = same(wg.at[:, lo, x], 4, to_r)
        l = same(wg.at[:, lo, x], 5, to_l)
        r.start()
        l.start()
        b_r.wait_recv()
        b_l.wait_recv()
        r2 = same(wg.at[yl, pl.ds(H, Q), xl], 6, to_r)
        l2 = same(wg.at[yl, pl.ds(H + Q, Q), xr], 7, to_l)
        r2.start()
        l2.start()
        return r, l, r2, l2

    def w_step3(r, l, r2, l2):
        r.wait_recv()
        l.wait_recv()
        r3 = same(wg.at[0, lo, xl], 8, to_r)
        l3 = same(wg.at[1, lo, xr], 9, to_l)
        r3.start()
        l3.start()
        r2.wait_recv()
        l2.wait_recv()
        y3 = same(wg.at[yl, hi], 10, to_y)
        y3.start()
        return r3, l3, y3

    wst = None
    wend = None
    for ph in range(PH):
        lanes = pl.ds(ph * PW, PW)
        pltpu.make_async_copy(recv.at[:, :, lanes], recv.at[:, :, lanes], in_r.at[ph]).wait()

        def col_head(h, _):
            hs = head_lanes(h)
            for i in range(C // B):
                rows, n = pl.ds(i * B, B), (i + 1) * B
                o, lse = attend(recv[0, rows, hs], recv[1, :n, hs], recv[2, :n, hs], bcol[rows, :n])
                ocs[rows, hs] = o.astype(bf16)
                put_lane(lcs, rows, h, lse)
            return 0

        lax.fori_loop(ph * HPP, (ph + 1) * HPP, col_head, 0)

        def back(i, _):
            p = (me + i) % SEQ
            rows = pl.ds(pl.multiple_of(p * TOK, TOK), TOK)
            rc(ocs.at[rows, lanes], ocr.at[mine, lanes], oc_s.at[ph], oc_r.at[ph], {"seq": p}).start()
            return 0

        lax.fori_loop(1, SEQ, back, 0)
        pltpu.make_async_copy(ocs.at[mine, lanes], ocr.at[mine, lanes], oc_r.at[ph]).start()
        if ph == 0:
            wst = w_step2()
        if ph == 2:
            wend = w_step3(*wst)

    def back_lse(i, _):
        p = (me + i) % SEQ
        rows = pl.ds(pl.multiple_of(p * TOK, TOK), TOK)
        rc(lcs.at[rows], lcr.at[mine], lc_s, lc_r, {"seq": p}).start()
        return 0

    lax.fori_loop(1, SEQ, back_lse, 0)
    pltpu.make_async_copy(lcs.at[mine], lcr.at[mine], lc_r).start()

    op.wait_recv()
    lp.wait_recv()
    pltpu.make_async_copy(lcr, lcr, lc_r).wait()

    l1 = lown[...]
    l2 = jnp.where(me > 0, lpr[...], NEG)
    l3 = lcr[...]
    top = jnp.maximum(jnp.maximum(l1, l2), l3)
    e1, e2, e3 = jnp.exp(l1 - top), jnp.exp(l2 - top), jnp.exp(l3 - top)
    inv = 1.0 / (e1 + e2 + e3)
    lown[...] = e1 * inv
    lpr[...] = e2 * inv
    lcr[...] = e3 * inv
    for ph in range(PH):
        lanes = pl.ds(ph * PW, PW)
        pltpu.make_async_copy(ocr.at[:, lanes], ocr.at[:, lanes], oc_r.at[ph]).wait()
        for h in range(ph * HPP, (ph + 1) * HPP):
            hs = pl.ds(h * HEAD, HEAD)
            g = (lown[:, h:h + 1] * oown[:, hs] + lpr[:, h:h + 1] * opr[:, hs].astype(f32)
                 + lcr[:, h:h + 1] * ocr[:, hs].astype(f32))
            att[:, hs] = g.astype(bf16)

    r3, l3_, y3 = wend
    r3.wait_recv()
    l3_.wait_recv()
    y3.wait_recv()

    ZC = NCH // NY
    ZW = NZ // ZC
    R = C // 4

    def to_core(n):
        return rc(cs.at[n], cr.at[n], c_s.at[n], c_r.at[n], core_peer)

    def to_ypeer(n):
        return rc(ys.at[n], yr.at[n], y_s.at[n], y_r.at[n], y_peer)

    def project(n):
        w = wg[n // ZC, pl.ds((n % ZC) * ZW, ZW)].reshape(CW, F)
        pr = lax.dot_general(att[...], w, (((1,), (1,)), ((), ())), preferred_element_type=f32)
        pr = pr.reshape(2, 2, R, CW)

        @pl.when(c == 0)
        def _():
            own[n] = pr[:, 0]
            cs[n] = pr[:, 1].astype(bf16)

        @pl.when(c == 1)
        def _():
            own[n] = pr[:, 1]
            cs[n] = pr[:, 0].astype(bf16)

        to_core(n).start()

    def across(n):
        to_core(n).wait_recv()
        ys[n] = (own[n, 1 - b] + cr[n, 1 - b].astype(f32)).astype(bf16)
        to_ypeer(n).start()

    def finish(n):
        to_ypeer(n).wait_recv()
        t = own[n, b] + cr[n, b].astype(f32) + yr[n].astype(f32)
        out[:, pl.ds(pl.multiple_of(n * CW, CW), CW)] = t.astype(bf16)

    project(0)

    def step(n, _):
        project(n)
        across(n - 1)
        return 0

    lax.fori_loop(1, NCH, step, 0)
    across(NCH - 1)

    def fin(n, _):
        finish(n)
        return 0

    lax.fori_loop(0, NCH, fin, 0)

    qcp.wait_send()
    op.wait_send()
    lp.wait_send()
    some = pl.ds(0, C - TOK)
    for ph in range(PH):
        lanes = pl.ds(ph * PW, PW)
        ref = qkv.at[:, some, lanes]
        pltpu.make_async_copy(ref, ref, in_s.at[ph]).wait()
        ref = ocs.at[some, lanes]
        pltpu.make_async_copy(ref, ref, oc_s.at[ph]).wait()
    pltpu.make_async_copy(lcs.at[some], lcs.at[some], lc_s).wait()
    part = wg.at[0, pl.ds(0, NZ - 1), 0]
    pltpu.make_async_copy(part, part, w_s.at[0]).wait()
    for cp in (a_y, b_r, b_l, *wst, *wend):
        cp.wait_send()

    def drain(n, _):
        to_core(n).wait_send()
        to_ypeer(n).wait_send()
        return 0

    lax.fori_loop(0, NCH, drain, 0)


def body(qkv, out_weight):
    qkv = qkv.reshape(3, C, F)
    wt = out_weight.T
    R = C // 4
    V, S = pltpu.VMEM, pltpu.SemaphoreType.DMA
    res = pl.pallas_call(
        kernel,
        out_shape=jax.ShapeDtypeStruct((R, D), bf16),
        in_specs=[pl.BlockSpec(memory_space=pl.ANY)] * 2,
        out_specs=pl.BlockSpec(memory_space=pltpu.VMEM),
        scratch_shapes=[
            V((3, C, F), bf16), V((3, C, F), bf16), V((C, F), bf16),
            V((C, F), bf16), V((C, 128), f32), V((C, F), bf16), V((C, 128), f32),
            V((C, F), bf16), V((C, 128), f32), V((C, F), bf16), V((C, 128), f32),
            V((C, F), f32), V((C, 128), f32),
            V((NY, NZ, NX, SLICE, F), bf16), V((C, F), bf16),
            V((C, C), f32), V((C, C), f32),
            V((NCH, 2, R, CW), bf16), V((NCH, 2, R, CW), bf16), V((NCH, 2, R, CW), f32),
            V((NCH, R, CW), bf16), V((NCH, R, CW), bf16),
            S((1,)), S((PH,)), S((PH,)), S, S, S((2,)), S((2,)), S((PH,)), S((PH,)),
            S, S, S((11,)), S((11,)), S((NCH,)), S((NCH,)), S((NCH,)), S((NCH,)),
        ],
        compiler_params=pltpu.CompilerParams(
            collective_id=0, has_side_effects=True, vmem_limit_bytes=60 * 1024 * 1024),
        name="attend_project",
    )(qkv, wt)
    return res.reshape(R, 1, D)


def solution(mesh):
    in_specs = (P(None, "seq", None, "head"), P("head", "seq"))
    out_specs = P("head", "seq", None)
    return jax.shard_map(body, mesh=mesh, in_specs=in_specs, out_specs=out_specs, check_vma=False)
```

```python
import functools

import jax
import jax.numpy as jnp
from jax import lax
from jax.experimental import pallas as pl
from jax.experimental.pallas import tpu as pltpu
from jax.sharding import PartitionSpec as P

MESH = pl.DeviceIdType.MESH
NY, NZ, NX = 2, 8, 4
SEQ = NY * NZ * NX
C = 512
F = 1024
HEAD = 128
HL = F // HEAD
D = 4096
SLICE = D // SEQ
TOK = C // SEQ
PH = 4
PW = F // PH
HPP = HL // PH
NCH = 8
CW = D // NCH
WC = 52
SCALE = HEAD ** -0.5
LOG2E = 1.4426950408889634
NEG = -1e30
f32 = jnp.float32
bf16 = jnp.bfloat16


def attend(q, k, v, bias):
    s = lax.dot_general(q, k, (((1,), (1,)), ((), ())), preferred_element_type=f32)
    if bias is not None:
        s = s + bias
    m = jnp.max(s, axis=1, keepdims=True)
    p = jnp.exp2((s - m) * (SCALE * LOG2E))
    l = jnp.sum(p, axis=1, keepdims=True)
    o = jnp.dot(p.astype(bf16), v, preferred_element_type=f32) * (1.0 / l)
    return o, m * SCALE + jnp.log(l)


def put_lane(ref, rows, h, val):
    lane = lax.broadcasted_iota(jnp.int32, (val.shape[0], 128), 1)
    ref[rows, :] = jnp.where(lane == h, val, ref[rows, :])


def split_lse(ref, dst):
    v = ref[...]
    hi = v.astype(bf16).astype(f32)
    lo = pltpu.roll((v - hi).astype(bf16).astype(f32), 64, 1)
    lane = lax.broadcasted_iota(jnp.int32, v.shape, 1)
    dst[...] = jnp.where(lane < 64, hi, lo).astype(bf16)


def join_lse(ref):
    v = ref[...].astype(f32)
    return v + pltpu.roll(v, 64, 1)


def kernel(qkv, qk6, wt, out, loc, recv, qn, ops, lps, opr, lpr, ocs, lcs, ocr, lcr, oown, lown, wg, att,
           bown, bcol, lpb, lcb, rq, ro, rq2, ro2, mid, midb, midl, m1, m2, m3, cs, cr, own, ys, yr, xs, xr2, ld_sem, iz_s, iz_r, ip_s, ip_r, bp_s, bp_r, bz_s, bz_r, q_s, q_r, rq_s, rq_r, ro_s, ro_r, rq2_s, rq2_r, ro2_s, ro2_r, op_s, op_r,
           w_s, w_r, c_s, c_r, y_s, y_r,
           x_s, x_r, at_s, at_r):
    me = lax.axis_index("seq")
    hd = lax.axis_index("head")
    yl, z, x = me // (NZ * NX), (me // NX) % NZ, me % NX
    b, c = hd // 2, hd % 2
    core_peer = {"head": b * 2 + (1 - c)}
    y_peer = {"head": (1 - b) * 2 + c}
    other = ((1 - yl) * NZ + z) * NX + x
    diag = {"seq": other, "head": (1 - b) * 2 + c}
    nxt, prv = (me + 1) % SEQ, (me + SEQ - 1) % SEQ

    def rc(src, dst, s, r, dev):
        return pltpu.make_async_remote_copy(src_ref=src, dst_ref=dst, send_sem=s, recv_sem=r,
                                            device_id=dev, device_id_type=MESH)

    barrier = pltpu.get_barrier_semaphore()

    def greet(i, _):
        pl.semaphore_signal(barrier, inc=1, device_id={"seq": (me + i) % SEQ}, device_id_type=MESH)
        return 0

    ld = pltpu.make_async_copy(qkv, loc, ld_sem.at[0])
    ld.start()
    lw = pltpu.make_async_copy(wt, wg.at[z, x], w_r.at[0])
    lw.start()
    lax.fori_loop(1, SEQ, greet, 0)
    pl.semaphore_signal(barrier, inc=1, device_id=core_peer, device_id_type=MESH)
    pl.semaphore_signal(barrier, inc=1, device_id=y_peer, device_id_type=MESH)
    pl.semaphore_signal(barrier, inc=1, device_id=diag, device_id_type=MESH)
    pl.semaphore_wait(barrier, SEQ + 2)

    quarter = pl.ds(pl.multiple_of(x * PW, PW), PW)

    @pl.when(x != 0)
    def _():
        rc(qkv.at[0], qn, q_s, q_r, {"seq": prv}).start()

    def part(j):
        return pl.ds(j * PW, PW)

    down = (me - x + SEQ - NX + x) % SEQ
    up = (me + NX) % SEQ
    q_up = {"seq": me - x + NX - 1}
    o_up = {"seq": me - x}

    @pl.when(x == 0)
    def _():
        for j in range(1, NX):
            rc(qkv.at[0, :, part(j)], rq, q_s, rq_r, {"seq": me + j}).start()
        rc(qkv.at[0, :, part(0)], rq2, q_s, rq2_r, {"seq": down}).start()

    q_z = rc(rq, rq2, rq_s, rq2_r, {"seq": down})
    q_zl = rc(rq, qn.at[:, part(NX - 1)], rq_s, q_r, {"seq": down})
    q_x = rc(rq2, qn.at[:, quarter], rq2_s, q_r, q_up)
    o_z = rc(ro, ro2, ro_s, ro2_r, {"seq": up})
    o_zl = rc(ro, opr.at[:, part(0)], ro_s, op_r.at[0], {"seq": up})
    o_x = rc(ro2, opr.at[:, quarter], ro2_s, op_r.at[0], o_up)

    xr, xl = (x + 1) % NX, (x + NX - 1) % NX
    to_r = {"seq": (yl * NZ + z) * NX + xr}
    to_l = {"seq": (yl * NZ + z) * NX + xl}
    to_u = {"seq": (yl * NZ + (z + 1) % NZ) * NX + x}
    to_d = {"seq": (yl * NZ + (z + NZ - 1) % NZ) * NX + x}
    count = [1]
    copies = {}

    def go(key, ref, dev, src=None):
        i = count[0]
        count[0] += 1
        copies[key] = rc(ref if src is None else src, ref, w_s.at[i], w_r.at[i], dev)
        copies[key].start()

    def got(*keys):
        for key in keys:
            copies[key].wait_recv()

    def at(o):
        return (z + o + NZ) % NZ

    HS = SLICE // 2
    h0, h1 = pl.ds(0, HS), pl.ds(HS, HS)

    def z_go(n):
        if n == 1:
            go(("u", 1), wg.at[z, x], to_u, wt)
            go(("d", 1), wg.at[z, x], to_d, wt)
        elif n < 4:
            go(("u", n), wg.at[at(1 - n), x], to_u)
            go(("d", n), wg.at[at(n - 1), x], to_d)
        else:
            go(("u", n), wg.at[at(-3), x, h0], to_u)
            go(("d", n), wg.at[at(3), x, h1], to_d)

    def z_got(n):
        got(("u", n), ("d", n))

    def br(*os):
        for o in os:
            go(("br", o), wg.at[at(o), x], to_r, wt if o == 0 else None)

    def bl(*os):
        for o in os:
            go(("bl", o), wg.at[at(o), x], to_l, wt if o == 0 else None)

    def bx2(*os):
        for o in os:
            got(("br", o), ("bl", o))
            go(("br2", o), wg.at[at(o), xl, h0], to_r)
            go(("bl2", o), wg.at[at(o), xr, h1], to_l)

    def x_got(*os):
        for o in os:
            got(("br2", o), ("bl2", o))

    def zring(n):
        z_got(n)
        if n < 4:
            z_go(n + 1)

    z_go(1)

    recv6 = recv.reshape(3, NY, NZ, NX, TOK, F)
    ocs6 = ocs.reshape(NY, NZ, NX, TOK, F)
    ocr6 = ocr.reshape(NY, NZ, NX, TOK, F)
    lcb6 = lcb.reshape(2, NY, NZ, NX, TOK, 128)
    lcr6 = lcr.reshape(2, NY, NZ, NX, TOK, 128)
    NP = NY * NX

    def lanes_of(ph):
        return pl.ds(ph * PW, PW)

    def each_z(src_of, dst, ss, rs):
        def one(i, _):
            p = (z + i) % NZ
            rc(src_of(p), dst, ss, rs, {"seq": (yl * NZ + p) * NX + x}).start()
            return 0

        lax.fori_loop(1, NZ, one, 0)
        pltpu.make_async_copy(src_of(z), dst, rs).start()

    def each_p(src_of, dst, ss, rs):
        def one(i, _):
            k = (yl * NX + x + i) % NP
            rc(src_of(k // NX, k % NX), dst, ss, rs, {"seq": ((k // NX) * NZ + z) * NX + k % NX}).start()
            return 0

        lax.fori_loop(1, NP, one, 0)
        pltpu.make_async_copy(src_of(yl, x), dst, rs).start()

    def await_all(ref, sem):
        pltpu.make_async_copy(ref, ref, sem).wait()

    def zin(ph):
        ln = lanes_of(ph)
        each_z(lambda p: qk6.at[:, :, p, :, :, ln], mid.at[:, z, :, :, :, ln], iz_s.at[ph], iz_r.at[ph])

    def pin(ph):
        ln = lanes_of(ph)
        await_all(mid.at[:, :, :, :, :, ln], iz_r.at[ph])
        each_p(lambda a, e: mid.at[:, :, a, e, :, ln], recv6.at[:, yl, :, x, :, ln], ip_s.at[ph], ip_r.at[ph])

    def bp(ph):
        ln = lanes_of(ph)
        each_p(lambda a, e: ocs6.at[a, :, e, :, ln], midb.at[:, yl, x, :, ln], bp_s.at[ph], bp_r.at[ph])

    def bz(ph):
        ln = lanes_of(ph)
        await_all(midb.at[:, :, :, :, ln], bp_r.at[ph])
        each_z(lambda p: midb.at[p, :, :, :, ln], ocr6.at[:, z, :, :, ln], bz_s.at[ph], bz_r.at[ph])

    def lse_p(g):
        split_lse(lcs, lcb.at[g])
        each_p(lambda a, e: lcb6.at[g, a, :, e], midl.at[g, :, yl, x], bp_s.at[PH + g], bp_r.at[PH + g])

    def lse_z(g):
        await_all(midl.at[g], bp_r.at[PH + g])
        each_z(lambda p: midl.at[g, p], lcr6.at[g, :, z], bz_s.at[PH + g], bz_r.at[PH + g])

    d = (lax.broadcasted_iota(jnp.int32, (C, C), 0) - lax.broadcasted_iota(jnp.int32, (C, C), 1))
    bown[...] = jnp.where(d >= 0, 0.0, NEG).astype(f32)
    bcol[...] = jnp.where((d >= 2 * TOK) & (d % TOK == 0), 0.0, NEG).astype(f32)
    lown[...] = jnp.zeros((C, 128), f32)
    lps[...] = jnp.zeros((C, 128), f32)
    lcs[...] = jnp.zeros((C, 128), f32)
    ld.wait()

    def head_lanes(h):
        return pl.ds(pl.multiple_of(h * HEAD, HEAD), HEAD)

    B = 256

    def own_head(h, _):
        hs = head_lanes(h)
        for i in range(C // B):
            rows, n = pl.ds(i * B, B), (i + 1) * B
            o, lse = attend(loc[0, rows, hs], loc[1, :n, hs], loc[2, :n, hs], bown[rows, :n])
            oown[rows, hs] = o
            put_lane(lown, rows, h, lse)
        return 0

    def q2():
        @pl.when(x != 0)
        def _():
            pltpu.make_async_copy(rq, rq, rq_r).wait()

        @pl.when((x != 0) & (x != NX - 1))
        def _():
            q_z.start()

        @pl.when(x == NX - 1)
        def _():
            q_zl.start()

    def q3():
        @pl.when(x != NX - 1)
        def _():
            pltpu.make_async_copy(rq2, rq2, rq2_r).wait()
            q_x.start()

    def o2():
        @pl.when(x != NX - 1)
        def _():
            pltpu.make_async_copy(ro, ro, ro_r).wait()

        @pl.when((x != 0) & (x != NX - 1))
        def _():
            o_z.start()

        @pl.when(x == 0)
        def _():
            o_zl.start()

    def o3():
        @pl.when(x != 0)
        def _():
            pltpu.make_async_copy(ro2, ro2, ro2_r).wait()
            o_x.start()

    def own_heads(a, e):
        lax.fori_loop(a, e, own_head, 0)


    def prev_head(h, _):
        hs = head_lanes(h)
        for i in range(C // B):
            rows = pl.ds(i * B, B)
            o, lse = attend(qn[rows, hs], loc[1, :, hs], loc[2, :, hs], None)
            ops[rows, hs] = o.astype(bf16)
            put_lane(lps, rows, h, lse)
        return 0

    def prev_heads(a, e):
        if a == 0:
            pltpu.make_async_copy(qn, qn, q_r).wait()
        lax.fori_loop(a, e, prev_head, 0)

    lp = rc(lpb, lpr, op_s.at[1], op_r.at[1], {"seq": nxt})

    def send_o():
        split_lse(lps, lpb)

        @pl.when(x != NX - 1)
        def _():
            rc(ops, opr, op_s.at[0], op_r.at[0], {"seq": nxt}).start()

        @pl.when(x == NX - 1)
        def _():
            for j in range(NX - 1):
                rc(ops.at[:, part(j)], ro, op_s.at[0], ro_r, {"seq": me - (NX - 1) + j}).start()
            rc(ops.at[:, part(NX - 1)], ro2, op_s.at[0], ro2_r, {"seq": up}).start()

        lp.start()

    def col(ph):
        await_all(recv.at[:, :, lanes_of(ph)], ip_r.at[ph])

        def col_head(h, _):
            hs = head_lanes(h)
            for i in range(C // B):
                rows, n = pl.ds(i * B, B), (i + 1) * B
                o, lse = attend(recv[0, rows, hs], recv[1, :n, hs], recv[2, :n, hs], bcol[rows, :n])
                ocs[rows, hs] = o.astype(bf16)
                put_lane(lcs, rows, h, lse)
            return 0

        lax.fori_loop(ph * HPP, (ph + 1) * HPP, col_head, 0)
        bp(ph)

    GW = F // 2
    peer = {"seq": other}

    def att_copy(g):
        ref = att.at[yl, :, pl.ds(g * GW, GW)]
        return rc(ref, ref, at_s.at[g], at_r.at[g], peer)

    def att_in(g):
        ref = att.at[1 - yl, :, pl.ds(g * GW, GW)]
        return rc(ref, ref, at_s.at[g], at_r.at[g], peer)

    def merge(g):
        if g == 0:
            await_all(opr, op_r.at[0])
            lp.wait_recv()
        await_all(lcr.at[g], bz_r.at[PH + g])
        l1 = lown[...]
        l2 = jnp.where(me > 0, join_lse(lpr), NEG)
        l3 = join_lse(lcr.at[g])
        top = jnp.maximum(jnp.maximum(l1, l2), l3)
        e1, e2, e3 = jnp.exp(l1 - top), jnp.exp(l2 - top), jnp.exp(l3 - top)
        inv = 1.0 / (e1 + e2 + e3)
        m1[...] = e1 * inv
        m2[...] = e2 * inv
        m3[...] = e3 * inv
        for ph in (2 * g, 2 * g + 1):
            await_all(ocr.at[:, lanes_of(ph)], bz_r.at[ph])
            for h in range(ph * HPP, (ph + 1) * HPP):
                hs = pl.ds(h * HEAD, HEAD)
                r = (m1[:, h:h + 1] * oown[:, hs] + m2[:, h:h + 1] * opr[:, hs].astype(f32)
                     + m3[:, h:h + 1] * ocr[:, hs].astype(f32))
                att[yl, :, hs] = r.astype(bf16)
        att_copy(g).start()

    lw.wait()
    own_heads(0, 3)
    zring(1)
    q2()
    br(0, -1, 1)
    own_heads(3, 6)
    zring(2)
    br(-2, 2)
    own_heads(6, 8)
    zring(3)
    q3()
    zin(0)
    br(-3, 3)
    zring(4)
    zin(1)
    br(4)
    prev_heads(0, 8)
    send_o()
    bl(0, -1, 1, -2, 2, -3, 3, 4)
    pin(0)
    zin(2)
    o2()
    bx2(0, -1, 1)
    pin(1)
    zin(3)
    col(0)
    o3()
    pin(2)
    bz(0)
    col(1)
    lse_p(0)
    bx2(-2, 2)
    bz(1)
    lse_z(0)
    pin(3)
    col(2)
    bx2(-3, 3, 4)
    bz(2)
    col(3)
    lse_p(1)
    bz(3)
    lse_z(1)
    merge(0)
    x_got(0, -1, 1, -2, 2, -3, 3, 4)
    merge(1)

    HC = NCH // 2
    ZW = NZ // HC
    R = C // 4

    def to_core(n):
        return rc(cs.at[n], cr.at[n], c_s.at[n], c_r.at[n], core_peer)

    def to_ypeer(n):
        return rc(ys.at[n], yr.at[n], y_s.at[n], y_r.at[n], y_peer)

    def to_side(m, k):
        dev = {"seq": other, "head": k * 2 + c}
        return rc(xs.at[m, k], xr2.at[m, b], x_s.at[m, k], x_r.at[m, b], dev)

    def project(n, m, row):
        w = wg[pl.ds(m * ZW, ZW)].reshape(CW, F)
        pr = lax.dot_general(att[row], w, (((1,), (1,)), ((), ())), preferred_element_type=f32)
        pr = pr.reshape(2, 2, R, CW)

        @pl.when(c == 0)
        def _():
            own[n] = pr[:, 0]
            cs[n] = pr[:, 1].astype(bf16)

        @pl.when(c == 1)
        def _():
            own[n] = pr[:, 1]
            cs[n] = pr[:, 0].astype(bf16)

        to_core(n).start()

    def across_own(n):
        to_core(n).wait_recv()
        ys[n] = (own[n, 1 - b] + cr[n, 1 - b].astype(f32)).astype(bf16)
        to_ypeer(n).start()

    def across_side(m):
        n = m + HC
        to_core(n).wait_recv()
        xs[m] = (own[n] + cr[n].astype(f32)).astype(bf16)
        to_side(m, 0).start()
        to_side(m, 1).start()

    def columns(half, m):
        return pl.ds(pl.multiple_of(half * (D // 2) + m * CW, CW), CW)

    def finish_own(n):
        to_ypeer(n).wait_recv()
        t = own[n, b] + cr[n, b].astype(f32) + yr[n].astype(f32)
        out[:, columns(yl, n)] = t.astype(bf16)

    def finish_side(m):
        for k in range(2):
            rc(xs.at[m, k], xr2.at[m, k], x_s.at[m, k], x_r.at[m, k], peer).wait_recv()
        t = xr2[m, 0].astype(f32) + xr2[m, 1].astype(f32)
        out[:, columns(1 - yl, m)] = t.astype(bf16)

    def loop(lo, hi, *fs):
        def one(n, _):
            for f in fs:
                f(n)
            return 0

        lax.fori_loop(lo, hi, one, 0)

    project(0, 0, yl)
    loop(1, HC, lambda n: project(n, n, yl), lambda n: across_own(n - 1))
    for g in range(2):
        att_in(g).wait_recv()
    project(HC, 0, 1 - yl)
    across_own(HC - 1)
    loop(1, HC, lambda m: project(m + HC, m, 1 - yl), lambda m: across_side(m - 1))
    across_side(HC - 1)
    loop(0, HC, finish_own)
    loop(0, HC, finish_side)

    pltpu.make_async_copy(qn, qn, q_s).wait()
    pltpu.make_async_copy(ops, ops, op_s.at[0]).wait()
    lp.wait_send()

    @pl.when(x != 0)
    def _():
        q_z.wait_send()
        o_x.wait_send()

    @pl.when(x != NX - 1)
    def _():
        o_z.wait_send()
        q_x.wait_send()

    seven = pl.ds(0, NZ - 1)
    for ph in range(PH):
        ln = lanes_of(ph)
        await_all(mid.at[:, seven, :, :, :, ln], iz_s.at[ph])
        await_all(mid.at[:, seven, :, :, :, ln], ip_s.at[ph])
        await_all(midb.at[seven, :, :, :, ln], bp_s.at[ph])
        await_all(midb.at[seven, :, :, :, ln], bz_s.at[ph])
    for g in range(2):
        await_all(midl.at[g, seven], bp_s.at[PH + g])
        await_all(midl.at[g, seven], bz_s.at[PH + g])
        att_copy(g).wait_send()
    for cp in copies.values():
        cp.wait_send()

    loop(0, NCH, lambda n: to_core(n).wait_send())
    loop(0, HC, lambda n: to_ypeer(n).wait_send())
    loop(0, HC, lambda m: to_side(m, 0).wait_send(), lambda m: to_side(m, 1).wait_send())


def body(qkv, out_weight):
    qkv = qkv.reshape(3, C, F)
    wt = out_weight.T
    R = C // 4
    V, S = pltpu.VMEM, pltpu.SemaphoreType.DMA
    res = pl.pallas_call(
        kernel,
        out_shape=jax.ShapeDtypeStruct((R, D), bf16),
        in_specs=[pl.BlockSpec(memory_space=pl.ANY)] * 3,
        out_specs=pl.BlockSpec(memory_space=pltpu.VMEM),
        scratch_shapes=[
            V((3, C, F), bf16), V((3, C, F), bf16), V((C, F), bf16),
            V((C, F), bf16), V((C, 128), f32), V((C, F), bf16), V((C, 128), bf16),
            V((C, F), bf16), V((C, 128), f32), V((C, F), bf16), V((2, C, 128), bf16),
            V((C, F), f32), V((C, 128), f32),
            V((NZ, NX, SLICE, F), bf16), V((NY, C, F), bf16),
            V((C, C), f32), V((C, C), f32),
            V((C, 128), bf16), V((2, C, 128), bf16), V((C, PW), bf16), V((C, PW), bf16), V((C, PW), bf16), V((C, PW), bf16),
            V((3, NZ, NY, NX, TOK, F), bf16), V((NZ, NY, NX, TOK, F), bf16), V((2, NZ, NY, NX, TOK, 128), bf16),
            V((C, 128), f32), V((C, 128), f32), V((C, 128), f32),
            V((NCH, 2, R, CW), bf16), V((NCH, 2, R, CW), bf16), V((NCH, 2, R, CW), f32),
            V((NCH // 2, R, CW), bf16), V((NCH // 2, R, CW), bf16),
            V((NCH // 2, 2, R, CW), bf16), V((NCH // 2, 2, R, CW), bf16),
            S((1,)), S((PH,)), S((PH,)), S((PH,)), S((PH,)), S((PH + 2,)), S((PH + 2,)), S((PH + 2,)), S((PH + 2,)),
            S, S, S, S, S, S, S, S, S, S, S((2,)), S((2,)),
            S((WC,)), S((WC,)), S((NCH,)), S((NCH,)), S((NCH // 2,)), S((NCH // 2,)),
            S((NCH // 2, 2)), S((NCH // 2, 2)), S((2,)), S((2,)),
        ],
        compiler_params=pltpu.CompilerParams(
            collective_id=0, has_side_effects=True, vmem_limit_bytes=60 * 1024 * 1024),
        name="attend_project",
    )(qkv, qkv.reshape(3, NY, NZ, NX, TOK, F), wt)
    return res.reshape(R, 1, D)


def solution(mesh):
    in_specs = (P(None, "seq", None, "head"), P("head", "seq"))
    out_specs = P("head", "seq", None)
    return jax.shard_map(body, mesh=mesh, in_specs=in_specs, out_specs=out_specs, check_vma=False)
```

```python
import functools

import jax
import jax.numpy as jnp
from jax import lax
from jax.experimental import pallas as pl
from jax.experimental.pallas import tpu as pltpu
from jax.sharding import PartitionSpec as P

MESH = pl.DeviceIdType.MESH
NY, NZ, NX = 2, 8, 4
SEQ = NY * NZ * NX
C = 512
F = 1024
HEAD = 128
HL = F // HEAD
D = 4096
SLICE = D // SEQ
TOK = C // SEQ
PH = 4
PW = F // PH
HPP = HL // PH
NCH = 8
CW = D // NCH
WC = 52
SCALE = HEAD ** -0.5
LOG2E = 1.4426950408889634
NEG = -1e30
f32 = jnp.float32
bf16 = jnp.bfloat16


def attend(q, k, v, bias):
    s = lax.dot_general(q, k, (((1,), (1,)), ((), ())), preferred_element_type=f32)
    if bias is not None:
        s = s + bias
    m = jnp.max(s, axis=1, keepdims=True)
    p = jnp.exp2((s - m) * (SCALE * LOG2E))
    l = jnp.sum(p, axis=1, keepdims=True)
    o = jnp.dot(p.astype(bf16), v, preferred_element_type=f32) * (1.0 / l)
    return o, m * SCALE + jnp.log(l)


def put_lane(ref, rows, h, val):
    lane = lax.broadcasted_iota(jnp.int32, (val.shape[0], 128), 1)
    ref[rows, :] = jnp.where(lane == h, val, ref[rows, :])


def split_lse(ref, dst):
    v = ref[...]
    hi = v.astype(bf16).astype(f32)
    lo = pltpu.roll((v - hi).astype(bf16).astype(f32), 64, 1)
    lane = lax.broadcasted_iota(jnp.int32, v.shape, 1)
    dst[...] = jnp.where(lane < 64, hi, lo).astype(bf16)


def join_lse(ref):
    v = ref[...].astype(f32)
    return v + pltpu.roll(v, 64, 1)


def kernel(qkv, qk6, wt, out, loc, recv, qn, ops, lps, opr, lpr, ocs, lcs, ocr, lcr, oown, lown, wg, att,
           bown, bcol, lpb, lcb, rq, ro, rq2, ro2, mid, midb, midl, m1, m2, m3, cs, cr, own, ys, yr, xs, xr2, ld_sem, iz_s, iz_r, ip_s, ip_r, bp_s, bp_r, bz_s, bz_r, q_s, q_r, rq_s, rq_r, ro_s, ro_r, rq2_s, rq2_r, ro2_s, ro2_r, op_s, op_r,
           w_s, w_r, c_s, c_r, y_s, y_r,
           x_s, x_r, at_s, at_r):
    me = lax.axis_index("seq")
    hd = lax.axis_index("head")
    yl, z, x = me // (NZ * NX), (me // NX) % NZ, me % NX
    b, c = hd // 2, hd % 2
    core_peer = {"head": b * 2 + (1 - c)}
    y_peer = {"head": (1 - b) * 2 + c}
    other = ((1 - yl) * NZ + z) * NX + x
    diag = {"seq": other, "head": (1 - b) * 2 + c}
    nxt, prv = (me + 1) % SEQ, (me + SEQ - 1) % SEQ

    def rc(src, dst, s, r, dev):
        return pltpu.make_async_remote_copy(src_ref=src, dst_ref=dst, send_sem=s, recv_sem=r,
                                            device_id=dev, device_id_type=MESH)

    barrier = pltpu.get_barrier_semaphore()

    def greet(i, _):
        pl.semaphore_signal(barrier, inc=1, device_id={"seq": (me + i) % SEQ}, device_id_type=MESH)
        return 0

    ld = pltpu.make_async_copy(qkv, loc, ld_sem.at[0])
    ld.start()
    lw = pltpu.make_async_copy(wt, wg.at[z, x], w_r.at[0])
    lw.start()
    lax.fori_loop(1, SEQ, greet, 0)
    pl.semaphore_signal(barrier, inc=1, device_id=core_peer, device_id_type=MESH)
    pl.semaphore_signal(barrier, inc=1, device_id=y_peer, device_id_type=MESH)
    pl.semaphore_signal(barrier, inc=1, device_id=diag, device_id_type=MESH)
    pl.semaphore_wait(barrier, SEQ + 2)

    quarter = pl.ds(pl.multiple_of(x * PW, PW), PW)

    @pl.when(x != 0)
    def _():
        rc(qkv.at[0], qn, q_s, q_r, {"seq": prv}).start()

    def part(j):
        return pl.ds(j * PW, PW)

    down = (me - x + SEQ - NX + x) % SEQ
    up = (me + NX) % SEQ
    q_up = {"seq": me - x + NX - 1}
    o_up = {"seq": me - x}

    @pl.when(x == 0)
    def _():
        for j in range(1, NX):
            rc(qkv.at[0, :, part(j)], rq, q_s, rq_r, {"seq": me + j}).start()
        rc(qkv.at[0, :, part(0)], rq2, q_s, rq2_r, {"seq": down}).start()

    q_z = rc(rq, rq2, rq_s, rq2_r, {"seq": down})
    q_zl = rc(rq, qn.at[:, part(NX - 1)], rq_s, q_r, {"seq": down})
    q_x = rc(rq2, qn.at[:, quarter], rq2_s, q_r, q_up)
    o_z = rc(ro, ro2, ro_s, ro2_r, {"seq": up})
    o_zl = rc(ro, opr.at[:, part(0)], ro_s, op_r.at[0], {"seq": up})
    o_x = rc(ro2, opr.at[:, quarter], ro2_s, op_r.at[0], o_up)

    xr, xl = (x + 1) % NX, (x + NX - 1) % NX
    to_r = {"seq": (yl * NZ + z) * NX + xr}
    to_l = {"seq": (yl * NZ + z) * NX + xl}
    to_u = {"seq": (yl * NZ + (z + 1) % NZ) * NX + x}
    to_d = {"seq": (yl * NZ + (z + NZ - 1) % NZ) * NX + x}
    count = [1]
    copies = {}

    def go(key, ref, dev, src=None):
        i = count[0]
        count[0] += 1
        copies[key] = rc(ref if src is None else src, ref, w_s.at[i], w_r.at[i], dev)
        copies[key].start()

    def got(*keys):
        for key in keys:
            copies[key].wait_recv()

    def at(o):
        return (z + o + NZ) % NZ

    HS = SLICE // 2
    h0, h1 = pl.ds(0, HS), pl.ds(HS, HS)

    def z_go(n):
        if n == 1:
            go(("u", 1), wg.at[z, x], to_u, wt)
            go(("d", 1), wg.at[z, x], to_d, wt)
        elif n < 4:
            go(("u", n), wg.at[at(1 - n), x], to_u)
            go(("d", n), wg.at[at(n - 1), x], to_d)
        else:
            go(("u", n), wg.at[at(-3), x, h0], to_u)
            go(("d", n), wg.at[at(3), x, h1], to_d)

    def z_got(n):
        got(("u", n), ("d", n))

    def br():
        go("br", wg.at[:, x], to_r)

    def bl():
        go("bl", wg.at[:, x], to_l)

    def bx2():
        got("br", "bl")
        go("br2", wg.at[:, xl, h0], to_r)
        go("bl2", wg.at[:, xr, h1], to_l)

    def x_got():
        got("br2", "bl2")

    def zring(n):
        z_got(n)
        if n < 4:
            z_go(n + 1)

    z_go(1)

    recv6 = recv.reshape(3, NY, NZ, NX, TOK, F)
    ocs6 = ocs.reshape(NY, NZ, NX, TOK, F)
    ocr6 = ocr.reshape(NY, NZ, NX, TOK, F)
    lcb6 = lcb.reshape(2, NY, NZ, NX, TOK, 128)
    lcr6 = lcr.reshape(2, NY, NZ, NX, TOK, 128)
    NP = NY * NX

    def lanes_of(ph):
        return pl.ds(ph * PW, PW)

    def each_z(src_of, dst, ss, rs):
        def one(i, _):
            p = (z + i) % NZ
            rc(src_of(p), dst, ss, rs, {"seq": (yl * NZ + p) * NX + x}).start()
            return 0

        lax.fori_loop(1, NZ, one, 0)
        pltpu.make_async_copy(src_of(z), dst, rs).start()

    def each_p(src_of, dst, ss, rs):
        def one(i, _):
            k = (yl * NX + x + i) % NP
            rc(src_of(k // NX, k % NX), dst, ss, rs, {"seq": ((k // NX) * NZ + z) * NX + k % NX}).start()
            return 0

        lax.fori_loop(1, NP, one, 0)
        pltpu.make_async_copy(src_of(yl, x), dst, rs).start()

    def await_all(ref, sem):
        pltpu.make_async_copy(ref, ref, sem).wait()

    def pin(ph):
        ln = lanes_of(ph)
        each_p(lambda a, e: qk6.at[:, a, :, e, :, ln], mid.at[:, :, yl, x, :, ln], ip_s.at[ph], ip_r.at[ph])

    def zin(ph):
        ln = lanes_of(ph)
        await_all(mid.at[:, :, :, :, :, ln], ip_r.at[ph])
        each_z(lambda p: mid.at[:, p, :, :, :, ln], recv6.at[:, :, z, :, :, ln], iz_s.at[ph], iz_r.at[ph])

    def bp(ph):
        ln = lanes_of(ph)
        each_p(lambda a, e: ocs6.at[a, :, e, :, ln], midb.at[:, yl, x, :, ln], bp_s.at[ph], bp_r.at[ph])

    def bz(ph):
        ln = lanes_of(ph)
        await_all(midb.at[:, :, :, :, ln], bp_r.at[ph])
        each_z(lambda p: midb.at[p, :, :, :, ln], ocr6.at[:, z, :, :, ln], bz_s.at[ph], bz_r.at[ph])

    def lse_p(g):
        split_lse(lcs, lcb.at[g])
        each_p(lambda a, e: lcb6.at[g, a, :, e], midl.at[g, :, yl, x], bp_s.at[PH + g], bp_r.at[PH + g])

    def lse_z(g):
        await_all(midl.at[g], bp_r.at[PH + g])
        each_z(lambda p: midl.at[g, p], lcr6.at[g, :, z], bz_s.at[PH + g], bz_r.at[PH + g])

    d = (lax.broadcasted_iota(jnp.int32, (C, C), 0) - lax.broadcasted_iota(jnp.int32, (C, C), 1))
    bown[...] = jnp.where(d >= 0, 0.0, NEG).astype(f32)
    bcol[...] = jnp.where((d >= 2 * TOK) & (d % TOK == 0), 0.0, NEG).astype(f32)
    lown[...] = jnp.zeros((C, 128), f32)
    lps[...] = jnp.zeros((C, 128), f32)
    lcs[...] = jnp.zeros((C, 128), f32)
    ld.wait()

    def head_lanes(h):
        return pl.ds(pl.multiple_of(h * HEAD, HEAD), HEAD)

    B = 256

    def own_head(h, _):
        hs = head_lanes(h)
        for i in range(C // B):
            rows, n = pl.ds(i * B, B), (i + 1) * B
            o, lse = attend(loc[0, rows, hs], loc[1, :n, hs], loc[2, :n, hs], bown[rows, :n])
            oown[rows, hs] = o
            put_lane(lown, rows, h, lse)
        return 0

    def q2():
        @pl.when(x != 0)
        def _():
            pltpu.make_async_copy(rq, rq, rq_r).wait()

        @pl.when((x != 0) & (x != NX - 1))
        def _():
            q_z.start()

        @pl.when(x == NX - 1)
        def _():
            q_zl.start()

    def q3():
        @pl.when(x != NX - 1)
        def _():
            pltpu.make_async_copy(rq2, rq2, rq2_r).wait()
            q_x.start()

    def o2():
        @pl.when(x != NX - 1)
        def _():
            pltpu.make_async_copy(ro, ro, ro_r).wait()

        @pl.when((x != 0) & (x != NX - 1))
        def _():
            o_z.start()

        @pl.when(x == 0)
        def _():
            o_zl.start()

    def o3():
        @pl.when(x != 0)
        def _():
            pltpu.make_async_copy(ro2, ro2, ro2_r).wait()
            o_x.start()

    def own_heads(a, e):
        lax.fori_loop(a, e, own_head, 0)


    def prev_head(h, _):
        hs = head_lanes(h)
        for i in range(C // B):
            rows = pl.ds(i * B, B)
            o, lse = attend(qn[rows, hs], loc[1, :, hs], loc[2, :, hs], None)
            ops[rows, hs] = o.astype(bf16)
            put_lane(lps, rows, h, lse)
        return 0

    def prev_heads(a, e):
        if a == 0:
            pltpu.make_async_copy(qn, qn, q_r).wait()
        lax.fori_loop(a, e, prev_head, 0)

    lp = rc(lpb, lpr, op_s.at[1], op_r.at[1], {"seq": nxt})

    def send_o():
        split_lse(lps, lpb)

        @pl.when(x != NX - 1)
        def _():
            rc(ops, opr, op_s.at[0], op_r.at[0], {"seq": nxt}).start()

        @pl.when(x == NX - 1)
        def _():
            for j in range(NX - 1):
                rc(ops.at[:, part(j)], ro, op_s.at[0], ro_r, {"seq": me - (NX - 1) + j}).start()
            rc(ops.at[:, part(NX - 1)], ro2, op_s.at[0], ro2_r, {"seq": up}).start()

        lp.start()

    def col(ph):
        await_all(recv.at[:, :, lanes_of(ph)], iz_r.at[ph])

        def col_head(h, _):
            hs = head_lanes(h)
            for i in range(C // B):
                rows, n = pl.ds(i * B, B), (i + 1) * B
                o, lse = attend(recv[0, rows, hs], recv[1, :n, hs], recv[2, :n, hs], bcol[rows, :n])
                ocs[rows, hs] = o.astype(bf16)
                put_lane(lcs, rows, h, lse)
            return 0

        lax.fori_loop(ph * HPP, (ph + 1) * HPP, col_head, 0)
        bp(ph)

    GROUPS = ((0, 1, 2), (3,))

    def group_lanes(g):
        return pl.ds(GROUPS[g][0] * PW, len(GROUPS[g]) * PW)

    peer = {"seq": other}

    def att_copy(g):
        ref = att.at[yl, :, group_lanes(g)]
        return rc(ref, ref, at_s.at[g], at_r.at[g], peer)

    def att_in(g):
        ref = att.at[1 - yl, :, group_lanes(g)]
        return rc(ref, ref, at_s.at[g], at_r.at[g], peer)

    def merge(g):
        if g == 0:
            await_all(opr, op_r.at[0])
            lp.wait_recv()
        await_all(lcr.at[g], bz_r.at[PH + g])
        l1 = lown[...]
        l2 = jnp.where(me > 0, join_lse(lpr), NEG)
        l3 = join_lse(lcr.at[g])
        top = jnp.maximum(jnp.maximum(l1, l2), l3)
        e1, e2, e3 = jnp.exp(l1 - top), jnp.exp(l2 - top), jnp.exp(l3 - top)
        inv = 1.0 / (e1 + e2 + e3)
        m1[...] = e1 * inv
        m2[...] = e2 * inv
        m3[...] = e3 * inv
        for ph in GROUPS[g]:
            await_all(ocr.at[:, lanes_of(ph)], bz_r.at[ph])
            for h in range(ph * HPP, (ph + 1) * HPP):
                hs = pl.ds(h * HEAD, HEAD)
                r = (m1[:, h:h + 1] * oown[:, hs] + m2[:, h:h + 1] * opr[:, hs].astype(f32)
                     + m3[:, h:h + 1] * ocr[:, hs].astype(f32))
                att[yl, :, hs] = r.astype(bf16)
        att_copy(g).start()

    pin(0)
    pin(1)
    pin(2)
    pin(3)
    lw.wait()
    own_heads(0, 3)
    zring(1)
    q2()
    own_heads(3, 6)
    zring(2)
    own_heads(6, 8)
    zring(3)
    q3()
    zring(4)
    zin(0)
    br()
    bl()
    zin(1)
    prev_heads(0, 8)
    send_o()
    zin(2)
    zin(3)
    col(0)
    bx2()
    o2()
    col(1)
    bz(0)
    o3()
    col(2)
    lse_p(0)
    bz(1)
    col(3)
    lse_p(1)
    bz(2)
    lse_z(0)
    bz(3)
    lse_z(1)
    merge(0)
    x_got()
    merge(1)

    HC = NCH // 2
    ZW = NZ // HC
    R = C // 4

    def to_core(n):
        return rc(cs.at[n], cr.at[n], c_s.at[n], c_r.at[n], core_peer)

    def to_ypeer(n):
        return rc(ys.at[n], yr.at[n], y_s.at[n], y_r.at[n], y_peer)

    def to_side(m, k):
        dev = {"seq": other, "head": k * 2 + c}
        return rc(xs.at[m, k], xr2.at[m, b], x_s.at[m, k], x_r.at[m, b], dev)

    def project(n, m, row):
        w = wg[pl.ds(m * ZW, ZW)].reshape(CW, F)
        pr = lax.dot_general(att[row], w, (((1,), (1,)), ((), ())), preferred_element_type=f32)
        pr = pr.reshape(2, 2, R, CW)

        @pl.when(c == 0)
        def _():
            own[n] = pr[:, 0]
            cs[n] = pr[:, 1].astype(bf16)

        @pl.when(c == 1)
        def _():
            own[n] = pr[:, 1]
            cs[n] = pr[:, 0].astype(bf16)

        to_core(n).start()

    def across_own(n):
        to_core(n).wait_recv()
        ys[n] = (own[n, 1 - b] + cr[n, 1 - b].astype(f32)).astype(bf16)
        to_ypeer(n).start()

    def across_side(m):
        n = m + HC
        to_core(n).wait_recv()
        xs[m] = (own[n] + cr[n].astype(f32)).astype(bf16)
        to_side(m, 0).start()
        to_side(m, 1).start()

    def columns(half, m):
        return pl.ds(pl.multiple_of(half * (D // 2) + m * CW, CW), CW)

    def finish_own(n):
        to_ypeer(n).wait_recv()
        t = own[n, b] + cr[n, b].astype(f32) + yr[n].astype(f32)
        out[:, columns(yl, n)] = t.astype(bf16)

    def finish_side(m):
        for k in range(2):
            rc(xs.at[m, k], xr2.at[m, k], x_s.at[m, k], x_r.at[m, k], peer).wait_recv()
        t = xr2[m, 0].astype(f32) + xr2[m, 1].astype(f32)
        out[:, columns(1 - yl, m)] = t.astype(bf16)

    def loop(lo, hi, *fs):
        def one(n, _):
            for f in fs:
                f(n)
            return 0

        lax.fori_loop(lo, hi, one, 0)

    project(0, 0, yl)
    loop(1, HC, lambda n: project(n, n, yl), lambda n: across_own(n - 1))
    for g in range(2):
        att_in(g).wait_recv()
    project(HC, 0, 1 - yl)
    across_own(HC - 1)
    loop(1, HC, lambda m: project(m + HC, m, 1 - yl), lambda m: across_side(m - 1))
    across_side(HC - 1)
    loop(0, HC, finish_own)
    loop(0, HC, finish_side)

    pltpu.make_async_copy(qn, qn, q_s).wait()
    pltpu.make_async_copy(ops, ops, op_s.at[0]).wait()
    lp.wait_send()

    @pl.when(x != 0)
    def _():
        q_z.wait_send()
        o_x.wait_send()

    @pl.when(x != NX - 1)
    def _():
        o_z.wait_send()
        q_x.wait_send()

    seven = pl.ds(0, NZ - 1)
    for ph in range(PH):
        ln = lanes_of(ph)
        await_all(mid.at[:, seven, :, :, :, ln], iz_s.at[ph])
        await_all(mid.at[:, seven, :, :, :, ln], ip_s.at[ph])
        await_all(midb.at[seven, :, :, :, ln], bp_s.at[ph])
        await_all(midb.at[seven, :, :, :, ln], bz_s.at[ph])
    for g in range(2):
        await_all(midl.at[g, seven], bp_s.at[PH + g])
        await_all(midl.at[g, seven], bz_s.at[PH + g])
        att_copy(g).wait_send()
    for cp in copies.values():
        cp.wait_send()

    loop(0, NCH, lambda n: to_core(n).wait_send())
    loop(0, HC, lambda n: to_ypeer(n).wait_send())
    loop(0, HC, lambda m: to_side(m, 0).wait_send(), lambda m: to_side(m, 1).wait_send())


def body(qkv, out_weight):
    qkv = qkv.reshape(3, C, F)
    wt = out_weight.T
    R = C // 4
    V, S = pltpu.VMEM, pltpu.SemaphoreType.DMA
    res = pl.pallas_call(
        kernel,
        out_shape=jax.ShapeDtypeStruct((R, D), bf16),
        in_specs=[pl.BlockSpec(memory_space=pl.ANY)] * 3,
        out_specs=pl.BlockSpec(memory_space=pltpu.VMEM),
        scratch_shapes=[
            V((3, C, F), bf16), V((3, C, F), bf16), V((C, F), bf16),
            V((C, F), bf16), V((C, 128), f32), V((C, F), bf16), V((C, 128), bf16),
            V((C, F), bf16), V((C, 128), f32), V((C, F), bf16), V((2, C, 128), bf16),
            V((C, F), f32), V((C, 128), f32),
            V((NZ, NX, SLICE, F), bf16), V((NY, C, F), bf16),
            V((C, C), f32), V((C, C), f32),
            V((C, 128), bf16), V((2, C, 128), bf16), V((C, PW), bf16), V((C, PW), bf16), V((C, PW), bf16), V((C, PW), bf16),
            V((3, NZ, NY, NX, TOK, F), bf16), V((NZ, NY, NX, TOK, F), bf16), V((2, NZ, NY, NX, TOK, 128), bf16),
            V((C, 128), f32), V((C, 128), f32), V((C, 128), f32),
            V((NCH, 2, R, CW), bf16), V((NCH, 2, R, CW), bf16), V((NCH, 2, R, CW), f32),
            V((NCH // 2, R, CW), bf16), V((NCH // 2, R, CW), bf16),
            V((NCH // 2, 2, R, CW), bf16), V((NCH // 2, 2, R, CW), bf16),
            S((1,)), S((PH,)), S((PH,)), S((PH,)), S((PH,)), S((PH + 2,)), S((PH + 2,)), S((PH + 2,)), S((PH + 2,)),
            S, S, S, S, S, S, S, S, S, S, S((2,)), S((2,)),
            S((WC,)), S((WC,)), S((NCH,)), S((NCH,)), S((NCH // 2,)), S((NCH // 2,)),
            S((NCH // 2, 2)), S((NCH // 2, 2)), S((2,)), S((2,)),
        ],
        compiler_params=pltpu.CompilerParams(
            collective_id=0, has_side_effects=True, vmem_limit_bytes=60 * 1024 * 1024),
        name="attend_project",
    )(qkv, qkv.reshape(3, NY, NZ, NX, TOK, F), wt)
    return res.reshape(R, 1, D)


def solution(mesh):
    in_specs = (P(None, "seq", None, "head"), P("head", "seq"))
    out_specs = P("head", "seq", None)
    return jax.shard_map(body, mesh=mesh, in_specs=in_specs, out_specs=out_specs, check_vma=False)
```

```python
import functools

import jax
import jax.numpy as jnp
from jax import lax
from jax.experimental import pallas as pl
from jax.experimental.pallas import tpu as pltpu
from jax.sharding import PartitionSpec as P

MESH = pl.DeviceIdType.MESH
NY, NZ, NX = 2, 8, 4
SEQ = NY * NZ * NX
C = 512
F = 1024
HEAD = 128
HL = F // HEAD
D = 4096
SLICE = D // SEQ
TOK = C // SEQ
PH = 4
PW = F // PH
HPP = HL // PH
NCH = 8
CW = D // NCH
WC = 52
SCALE = HEAD ** -0.5
LOG2E = 1.4426950408889634
NEG = -1e30
f32 = jnp.float32
bf16 = jnp.bfloat16


def attend(q, k, v, bias):
    s = lax.dot_general(q, k, (((1,), (1,)), ((), ())), preferred_element_type=f32)
    if bias is not None:
        s = s + bias
    m = jnp.max(s, axis=1, keepdims=True)
    p = jnp.exp2((s - m) * (SCALE * LOG2E))
    l = jnp.sum(p, axis=1, keepdims=True)
    o = jnp.dot(p.astype(bf16), v, preferred_element_type=f32) * (1.0 / l)
    return o, m * SCALE + jnp.log(l)


def put_lane(ref, rows, h, val):
    lane = lax.broadcasted_iota(jnp.int32, (val.shape[0], 128), 1)
    ref[rows, :] = jnp.where(lane == h, val, ref[rows, :])


def split_lse(ref, dst):
    v = ref[...]
    hi = v.astype(bf16).astype(f32)
    lo = pltpu.roll((v - hi).astype(bf16).astype(f32), 64, 1)
    lane = lax.broadcasted_iota(jnp.int32, v.shape, 1)
    dst[...] = jnp.where(lane < 64, hi, lo).astype(bf16)


def join_lse(ref):
    v = ref[...].astype(f32)
    return v + pltpu.roll(v, 64, 1)


def kernel(qkv, qk6, wt, out, loc, recv, qn, ops, lps, opr, lpr, ocs, lcs, ocr, lcr, oown, lown, wg, att,
           bown, bcol, lpb, lcb, rq, ro, rq2, ro2, mid, midb, midl, m1, m2, m3, cs, cr, own, ys, yr, xs, xr2, ld_sem, iz_s, iz_r, ip_s, ip_r, bp_s, bp_r, bz_s, bz_r, q_s, q_r, rq_s, rq_r, ro_s, ro_r, rq2_s, rq2_r, ro2_s, ro2_r, op_s, op_r,
           w_s, w_r, c_s, c_r, y_s, y_r,
           x_s, x_r, at_s, at_r):
    me = lax.axis_index("seq")
    hd = lax.axis_index("head")
    yl, z, x = me // (NZ * NX), (me // NX) % NZ, me % NX
    b, c = hd // 2, hd % 2
    core_peer = {"head": b * 2 + (1 - c)}
    y_peer = {"head": (1 - b) * 2 + c}
    other = ((1 - yl) * NZ + z) * NX + x
    diag = {"seq": other, "head": (1 - b) * 2 + c}
    nxt, prv = (me + 1) % SEQ, (me + SEQ - 1) % SEQ

    def rc(src, dst, s, r, dev):
        return pltpu.make_async_remote_copy(src_ref=src, dst_ref=dst, send_sem=s, recv_sem=r,
                                            device_id=dev, device_id_type=MESH)

    barrier = pltpu.get_barrier_semaphore()

    def greet(i, _):
        pl.semaphore_signal(barrier, inc=1, device_id={"seq": (me + i) % SEQ}, device_id_type=MESH)
        return 0

    ld = pltpu.make_async_copy(qkv, loc, ld_sem.at[0])
    ld.start()
    lw = pltpu.make_async_copy(wt, wg.at[z, x], w_r.at[0])
    lw.start()
    lax.fori_loop(1, SEQ, greet, 0)
    pl.semaphore_signal(barrier, inc=1, device_id=core_peer, device_id_type=MESH)
    pl.semaphore_signal(barrier, inc=1, device_id=y_peer, device_id_type=MESH)
    pl.semaphore_signal(barrier, inc=1, device_id=diag, device_id_type=MESH)
    pl.semaphore_wait(barrier, SEQ + 2)

    quarter = pl.ds(pl.multiple_of(x * PW, PW), PW)

    @pl.when(x != 0)
    def _():
        rc(qkv.at[0], qn, q_s, q_r, {"seq": prv}).start()

    def part(j):
        return pl.ds(j * PW, PW)

    down = (me - x + SEQ - NX + x) % SEQ
    up = (me + NX) % SEQ
    q_up = {"seq": me - x + NX - 1}
    o_up = {"seq": me - x}

    @pl.when(x == 0)
    def _():
        for j in range(1, NX):
            rc(qkv.at[0, :, part(j)], rq, q_s, rq_r, {"seq": me + j}).start()
        rc(qkv.at[0, :, part(0)], rq2, q_s, rq2_r, {"seq": down}).start()

    q_z = rc(rq, rq2, rq_s, rq2_r, {"seq": down})
    q_zl = rc(rq, qn.at[:, part(NX - 1)], rq_s, q_r, {"seq": down})
    q_x = rc(rq2, qn.at[:, quarter], rq2_s, q_r, q_up)
    o_z = rc(ro, ro2, ro_s, ro2_r, {"seq": up})
    o_zl = rc(ro, opr.at[:, part(0)], ro_s, op_r.at[0], {"seq": up})
    o_x = rc(ro2, opr.at[:, quarter], ro2_s, op_r.at[0], o_up)

    xr, xl = (x + 1) % NX, (x + NX - 1) % NX
    to_r = {"seq": (yl * NZ + z) * NX + xr}
    to_l = {"seq": (yl * NZ + z) * NX + xl}
    to_u = {"seq": (yl * NZ + (z + 1) % NZ) * NX + x}
    to_d = {"seq": (yl * NZ + (z + NZ - 1) % NZ) * NX + x}
    count = [1]
    copies = {}

    def go(key, ref, dev, src=None):
        i = count[0]
        count[0] += 1
        copies[key] = rc(ref if src is None else src, ref, w_s.at[i], w_r.at[i], dev)
        copies[key].start()

    def got(*keys):
        for key in keys:
            copies[key].wait_recv()

    def at(o):
        return (z + o + NZ) % NZ

    HS = SLICE // 2
    h0, h1 = pl.ds(0, HS), pl.ds(HS, HS)

    def z_go(n):
        if n == 1:
            go(("u", 1), wg.at[z, x], to_u, wt)
            go(("d", 1), wg.at[z, x], to_d, wt)
        elif n < 4:
            go(("u", n), wg.at[at(1 - n), x], to_u)
            go(("d", n), wg.at[at(n - 1), x], to_d)
        else:
            go(("u", n), wg.at[at(-3), x, h0], to_u)
            go(("d", n), wg.at[at(3), x, h1], to_d)

    def z_got(n):
        got(("u", n), ("d", n))

    def br():
        go("br", wg.at[:, x], to_r)

    def bl():
        go("bl", wg.at[:, x], to_l)

    def bx2():
        got("br", "bl")
        go("br2", wg.at[:, xl, h0], to_r)
        go("bl2", wg.at[:, xr, h1], to_l)

    def x_got():
        got("br2", "bl2")

    def zring(n):
        z_got(n)
        if n < 4:
            z_go(n + 1)

    z_go(1)

    recv6 = recv.reshape(3, NY, NZ, NX, TOK, F)
    ocs6 = ocs.reshape(NY, NZ, NX, TOK, F)
    ocr6 = ocr.reshape(NY, NZ, NX, TOK, F)
    lcb6 = lcb.reshape(2, NY, NZ, NX, TOK, 128)
    lcr6 = lcr.reshape(2, NY, NZ, NX, TOK, 128)
    NP = NY * NX

    def lanes_of(ph):
        return pl.ds(ph * PW, PW)

    def each_z(src_of, dst, ss, rs):
        def one(i, _):
            p = (z + i) % NZ
            rc(src_of(p), dst, ss, rs, {"seq": (yl * NZ + p) * NX + x}).start()
            return 0

        lax.fori_loop(1, NZ, one, 0)
        pltpu.make_async_copy(src_of(z), dst, rs).start()

    def each_p(src_of, dst, ss, rs):
        def one(i, _):
            k = (yl * NX + x + i) % NP
            rc(src_of(k // NX, k % NX), dst, ss, rs, {"seq": ((k // NX) * NZ + z) * NX + k % NX}).start()
            return 0

        lax.fori_loop(1, NP, one, 0)
        pltpu.make_async_copy(src_of(yl, x), dst, rs).start()

    def await_all(ref, sem):
        pltpu.make_async_copy(ref, ref, sem).wait()

    def pin(ph):
        ln = lanes_of(ph)
        each_p(lambda a, e: qk6.at[:, a, :, e, :, ln], mid.at[:, :, yl, x, :, ln], ip_s.at[ph], ip_r.at[ph])

    def zin(ph):
        ln = lanes_of(ph)
        await_all(mid.at[:, :, :, :, :, ln], ip_r.at[ph])
        each_z(lambda p: mid.at[:, p, :, :, :, ln], recv6.at[:, :, z, :, :, ln], iz_s.at[ph], iz_r.at[ph])

    def bp(ph):
        ln = lanes_of(ph)
        each_p(lambda a, e: ocs6.at[a, :, e, :, ln], midb.at[:, yl, x, :, ln], bp_s.at[ph], bp_r.at[ph])

    def bz(ph):
        ln = lanes_of(ph)
        await_all(midb.at[:, :, :, :, ln], bp_r.at[ph])
        each_z(lambda p: midb.at[p, :, :, :, ln], ocr6.at[:, z, :, :, ln], bz_s.at[ph], bz_r.at[ph])

    def lse_p(g):
        split_lse(lcs, lcb.at[g])
        each_p(lambda a, e: lcb6.at[g, a, :, e], midl.at[g, :, yl, x], bp_s.at[PH + g], bp_r.at[PH + g])

    def lse_z(g):
        await_all(midl.at[g], bp_r.at[PH + g])
        each_z(lambda p: midl.at[g, p], lcr6.at[g, :, z], bz_s.at[PH + g], bz_r.at[PH + g])

    d = (lax.broadcasted_iota(jnp.int32, (C, C), 0) - lax.broadcasted_iota(jnp.int32, (C, C), 1))
    bown[...] = jnp.where(d >= 0, 0.0, NEG).astype(f32)
    bcol[...] = jnp.where((d >= 2 * TOK) & (d % TOK == 0), 0.0, NEG).astype(f32)
    lown[...] = jnp.zeros((C, 128), f32)
    lps[...] = jnp.zeros((C, 128), f32)
    lcs[...] = jnp.zeros((C, 128), f32)
    ld.wait()

    def head_lanes(h):
        return pl.ds(pl.multiple_of(h * HEAD, HEAD), HEAD)

    B = 256

    def own_head(h, _):
        hs = head_lanes(h)
        for i in range(C // B):
            rows, n = pl.ds(i * B, B), (i + 1) * B
            o, lse = attend(loc[0, rows, hs], loc[1, :n, hs], loc[2, :n, hs], bown[rows, :n])
            oown[rows, hs] = o
            put_lane(lown, rows, h, lse)
        return 0

    def q2():
        @pl.when(x != 0)
        def _():
            pltpu.make_async_copy(rq, rq, rq_r).wait()

        @pl.when((x != 0) & (x != NX - 1))
        def _():
            q_z.start()

        @pl.when(x == NX - 1)
        def _():
            q_zl.start()

    def q3():
        @pl.when(x != NX - 1)
        def _():
            pltpu.make_async_copy(rq2, rq2, rq2_r).wait()
            q_x.start()

    def o2():
        @pl.when(x != NX - 1)
        def _():
            pltpu.make_async_copy(ro, ro, ro_r).wait()

        @pl.when((x != 0) & (x != NX - 1))
        def _():
            o_z.start()

        @pl.when(x == 0)
        def _():
            o_zl.start()

    def o3():
        @pl.when(x != 0)
        def _():
            pltpu.make_async_copy(ro2, ro2, ro2_r).wait()
            o_x.start()

    def own_heads(a, e):
        lax.fori_loop(a, e, own_head, 0)


    def prev_head(h, _):
        hs = head_lanes(h)
        for i in range(C // B):
            rows = pl.ds(i * B, B)
            o, lse = attend(qn[rows, hs], loc[1, :, hs], loc[2, :, hs], None)
            ops[rows, hs] = o.astype(bf16)
            put_lane(lps, rows, h, lse)
        return 0

    def prev_heads(a, e):
        if a == 0:
            pltpu.make_async_copy(qn, qn, q_r).wait()
        lax.fori_loop(a, e, prev_head, 0)

    lp = rc(lpb, lpr, op_s.at[1], op_r.at[1], {"seq": nxt})

    def send_o():
        split_lse(lps, lpb)

        @pl.when(x != NX - 1)
        def _():
            rc(ops, opr, op_s.at[0], op_r.at[0], {"seq": nxt}).start()

        @pl.when(x == NX - 1)
        def _():
            for j in range(NX - 1):
                rc(ops.at[:, part(j)], ro, op_s.at[0], ro_r, {"seq": me - (NX - 1) + j}).start()
            rc(ops.at[:, part(NX - 1)], ro2, op_s.at[0], ro2_r, {"seq": up}).start()

        lp.start()

    def col(ph):
        await_all(recv.at[:, :, lanes_of(ph)], iz_r.at[ph])

        def col_head(h, _):
            hs = head_lanes(h)
            for i in range(C // B):
                rows, n = pl.ds(i * B, B), (i + 1) * B
                o, lse = attend(recv[0, rows, hs], recv[1, :n, hs], recv[2, :n, hs], bcol[rows, :n])
                ocs[rows, hs] = o.astype(bf16)
                put_lane(lcs, rows, h, lse)
            return 0

        lax.fori_loop(ph * HPP, (ph + 1) * HPP, col_head, 0)
        bp(ph)

    GROUPS = ((0, 1, 2), (3,))

    def group_lanes(g):
        return pl.ds(GROUPS[g][0] * PW, len(GROUPS[g]) * PW)

    peer = {"seq": other}

    def att_copy(g):
        ref = att.at[yl, :, group_lanes(g)]
        return rc(ref, ref, at_s.at[g], at_r.at[g], peer)

    def att_in(g):
        ref = att.at[1 - yl, :, group_lanes(g)]
        return rc(ref, ref, at_s.at[g], at_r.at[g], peer)

    def merge(g):
        if g == 0:
            await_all(opr, op_r.at[0])
            lp.wait_recv()
        await_all(lcr.at[g], bz_r.at[PH + g])
        l1 = lown[...]
        l2 = jnp.where(me > 0, join_lse(lpr), NEG)
        l3 = join_lse(lcr.at[g])
        top = jnp.maximum(jnp.maximum(l1, l2), l3)
        e1, e2, e3 = jnp.exp(l1 - top), jnp.exp(l2 - top), jnp.exp(l3 - top)
        inv = 1.0 / (e1 + e2 + e3)
        m1[...] = e1 * inv
        m2[...] = e2 * inv
        m3[...] = e3 * inv
        for ph in GROUPS[g]:
            await_all(ocr.at[:, lanes_of(ph)], bz_r.at[ph])
            for h in range(ph * HPP, (ph + 1) * HPP):
                hs = pl.ds(h * HEAD, HEAD)
                r = (m1[:, h:h + 1] * oown[:, hs] + m2[:, h:h + 1] * opr[:, hs].astype(f32)
                     + m3[:, h:h + 1] * ocr[:, hs].astype(f32))
                att[yl, :, hs] = r.astype(bf16)
        att_copy(g).start()

    pin(0)
    pin(1)
    pin(2)
    pin(3)
    lw.wait()
    own_heads(0, 3)
    zring(1)
    q2()
    own_heads(3, 6)
    zring(2)
    own_heads(6, 8)
    zring(3)
    q3()
    zring(4)
    zin(0)
    br()
    bl()
    zin(1)
    prev_heads(0, 8)
    send_o()
    zin(2)
    zin(3)
    col(0)
    bx2()
    o2()
    col(1)
    bz(0)
    o3()
    col(2)
    lse_p(0)
    bz(1)
    col(3)
    lse_p(1)
    bz(2)
    lse_z(0)
    bz(3)
    lse_z(1)
    merge(0)
    x_got()
    merge(1)

    HC = NCH // 2
    ZW = NZ // HC
    R = C // 4

    def to_core(n):
        return rc(cs.at[n], cr.at[n], c_s.at[n], c_r.at[n], core_peer)

    def to_ypeer(n):
        return rc(ys.at[n], yr.at[n], y_s.at[n], y_r.at[n], y_peer)

    def to_side(m, k):
        dev = {"seq": other, "head": k * 2 + c}
        return rc(xs.at[m, k], xr2.at[m, b], x_s.at[m, k], x_r.at[m, b], dev)

    def project(n, m, row):
        w = wg[pl.ds(m * ZW, ZW)].reshape(CW, F)
        pr = lax.dot_general(att[row], w, (((1,), (1,)), ((), ())), preferred_element_type=f32)
        pr = pr.reshape(2, 2, R, CW)

        @pl.when(c == 0)
        def _():
            own[n] = pr[:, 0]
            cs[n] = pr[:, 1].astype(bf16)

        @pl.when(c == 1)
        def _():
            own[n] = pr[:, 1]
            cs[n] = pr[:, 0].astype(bf16)

        to_core(n).start()

    def across_own(n):
        to_core(n).wait_recv()
        ys[n] = (own[n, 1 - b] + cr[n, 1 - b].astype(f32)).astype(bf16)
        to_ypeer(n).start()

    def across_side(m):
        n = m + HC
        to_core(n).wait_recv()
        xs[m] = (own[n] + cr[n].astype(f32)).astype(bf16)
        to_side(m, 0).start()
        to_side(m, 1).start()

    def columns(half, m):
        return pl.ds(pl.multiple_of(half * (D // 2) + m * CW, CW), CW)

    def finish_own(n):
        to_ypeer(n).wait_recv()
        t = own[n, b] + cr[n, b].astype(f32) + yr[n].astype(f32)
        out[:, columns(yl, n)] = t.astype(bf16)

    def finish_side(m):
        for k in range(2):
            rc(xs.at[m, k], xr2.at[m, k], x_s.at[m, k], x_r.at[m, k], peer).wait_recv()
        t = xr2[m, 0].astype(f32) + xr2[m, 1].astype(f32)
        out[:, columns(1 - yl, m)] = t.astype(bf16)

    def loop(lo, hi, *fs):
        def one(n, _):
            for f in fs:
                f(n)
            return 0

        lax.fori_loop(lo, hi, one, 0)

    project(0, 0, yl)
    loop(1, HC, lambda n: project(n, n, yl), lambda n: across_own(n - 1))
    for g in range(2):
        att_in(g).wait_recv()
    project(HC, 0, 1 - yl)
    across_own(HC - 1)
    loop(1, HC, lambda m: project(m + HC, m, 1 - yl), lambda m: across_side(m - 1),
         lambda m: finish_own(m - 1))
    across_side(HC - 1)
    finish_own(HC - 1)
    loop(0, HC, finish_side)

    pltpu.make_async_copy(qn, qn, q_s).wait()
    pltpu.make_async_copy(ops, ops, op_s.at[0]).wait()
    lp.wait_send()

    @pl.when(x != 0)
    def _():
        q_z.wait_send()
        o_x.wait_send()

    @pl.when(x != NX - 1)
    def _():
        o_z.wait_send()
        q_x.wait_send()

    seven = pl.ds(0, NZ - 1)
    for ph in range(PH):
        ln = lanes_of(ph)
        await_all(mid.at[:, seven, :, :, :, ln], iz_s.at[ph])
        await_all(mid.at[:, seven, :, :, :, ln], ip_s.at[ph])
        await_all(midb.at[seven, :, :, :, ln], bp_s.at[ph])
        await_all(midb.at[seven, :, :, :, ln], bz_s.at[ph])
    for g in range(2):
        await_all(midl.at[g, seven], bp_s.at[PH + g])
        await_all(midl.at[g, seven], bz_s.at[PH + g])
        att_copy(g).wait_send()
    for cp in copies.values():
        cp.wait_send()

    loop(0, NCH, lambda n: to_core(n).wait_send())
    loop(0, HC, lambda n: to_ypeer(n).wait_send())
    loop(0, HC, lambda m: to_side(m, 0).wait_send(), lambda m: to_side(m, 1).wait_send())


def body(qkv, out_weight):
    qkv = qkv.reshape(3, C, F)
    wt = out_weight.T
    R = C // 4
    V, S = pltpu.VMEM, pltpu.SemaphoreType.DMA
    res = pl.pallas_call(
        kernel,
        out_shape=jax.ShapeDtypeStruct((R, D), bf16),
        in_specs=[pl.BlockSpec(memory_space=pl.ANY)] * 3,
        out_specs=pl.BlockSpec(memory_space=pltpu.VMEM),
        scratch_shapes=[
            V((3, C, F), bf16), V((3, C, F), bf16), V((C, F), bf16),
            V((C, F), bf16), V((C, 128), f32), V((C, F), bf16), V((C, 128), bf16),
            V((C, F), bf16), V((C, 128), f32), V((C, F), bf16), V((2, C, 128), bf16),
            V((C, F), f32), V((C, 128), f32),
            V((NZ, NX, SLICE, F), bf16), V((NY, C, F), bf16),
            V((C, C), f32), V((C, C), f32),
            V((C, 128), bf16), V((2, C, 128), bf16), V((C, PW), bf16), V((C, PW), bf16), V((C, PW), bf16), V((C, PW), bf16),
            V((3, NZ, NY, NX, TOK, F), bf16), V((NZ, NY, NX, TOK, F), bf16), V((2, NZ, NY, NX, TOK, 128), bf16),
            V((C, 128), f32), V((C, 128), f32), V((C, 128), f32),
            V((NCH, 2, R, CW), bf16), V((NCH, 2, R, CW), bf16), V((NCH, 2, R, CW), f32),
            V((NCH // 2, R, CW), bf16), V((NCH // 2, R, CW), bf16),
            V((NCH // 2, 2, R, CW), bf16), V((NCH // 2, 2, R, CW), bf16),
            S((1,)), S((PH,)), S((PH,)), S((PH,)), S((PH,)), S((PH + 2,)), S((PH + 2,)), S((PH + 2,)), S((PH + 2,)),
            S, S, S, S, S, S, S, S, S, S, S((2,)), S((2,)),
            S((WC,)), S((WC,)), S((NCH,)), S((NCH,)), S((NCH // 2,)), S((NCH // 2,)),
            S((NCH // 2, 2)), S((NCH // 2, 2)), S((2,)), S((2,)),
        ],
        compiler_params=pltpu.CompilerParams(
            collective_id=0, has_side_effects=True, vmem_limit_bytes=60 * 1024 * 1024),
        name="attend_project",
    )(qkv, qkv.reshape(3, NY, NZ, NX, TOK, F), wt)
    return res.reshape(R, 1, D)


def solution(mesh):
    in_specs = (P(None, "seq", None, "head"), P("head", "seq"))
    out_specs = P("head", "seq", None)
    return jax.shard_map(body, mesh=mesh, in_specs=in_specs, out_specs=out_specs, check_vma=False)
```
